512 devices in a mesh: leaf: 32 (over z, core), bond: 16 (over x, y).
Axes of the slice: x: 4, y: 4, z: 16, core: 2. Of those that a mesh axis runs over, the one named last changes fastest.
Arguments:
- isometries: bfloat16 [32, 256, 256, 256], P('leaf', 'bond'), may hold values from -0.1875 to 0.1875
- leaf_ops: bfloat16 [32, 1, 256, 256], P('leaf', None, 'bond'), may hold values from -6 to 6
- charges: int32 [32, 3, 4], P('leaf'), may hold values from 0 to 3
- assign: int32 [32, 1], P('leaf'), may hold values from 0 to 2
Outputs:
- node_ops: bfloat16 [32, 1, 256, 256], P('leaf', None, 'bond')
The draws below stay inside these ranges and needn't reach their ends.
Inputs may be any that keep to these rules, and one draw needn't show every extreme that they name: `assign`: 0 takes the left child's operator, 1 the right child's, 2 their sum.
All inputs are finite; a program needn't handle non-finite values.
Results may differ from the reference program's by a relative error of at most 0.008.
Values may be sent and summed in bfloat16 or wider, within the bound.
A program may use at most 64 MiB of HBM per device.

```python
import jax
import jax.numpy as jnp
from jax import lax

CHI = 256
BLOCK = 64
QMOD = 4
OPS = 1
LEVELS = 3
NBLK = 4
SLOTS = 32


def touch_ends(values, stream_key, least, largest):
    spot = [jax.random.randint(jax.random.fold_in(stream_key, axis), (), 0, length) for axis, length in enumerate(values.shape)]
    main_axis = values.shape.index(max(values.shape))
    beside = spot[:main_axis] + [(spot[main_axis] + 1) % values.shape[main_axis]] + spot[main_axis + 1:]
    return values.at[tuple(spot)].set(least).at[tuple(beside)].set(largest)


def levels(key, dims, split, least, largest):
    gain = 1.0
    for axis_at, shards_of in split:
        draws = jax.random.uniform(jax.random.fold_in(jax.random.fold_in(key, 6), axis_at), (shards_of,), jnp.float32, least / len(split), largest / len(split))
        gain = gain * jnp.repeat(jnp.exp(draws), dims[axis_at] // shards_of).reshape((-1,) + (1,) * (len(dims) - 1 - axis_at))
    return gain


def gaussian(rng, dims, scale, reach, pieces=(), kind=jnp.bfloat16):
    gain = levels(rng, dims, pieces, -0.22, 0.18) if pieces else 1.0
    values = jax.random.normal(rng, dims, jnp.float32) * scale * gain
    return jnp.minimum(jnp.maximum(values, -reach), reach).astype(kind)


def setup_inputs(seed: int = 0) -> dict:
    splits = jax.random.split(jax.random.key(seed), 5)
    return {
        "isometries": gaussian(splits[0], (SLOTS, CHI, CHI, CHI), (4 * CHI) ** -0.5, 0.1875, ((0, 32), (1, 16))),
        "leaf_ops": gaussian(splits[1], (SLOTS, OPS, CHI, CHI), 1.0, 6.0, ((0, 32), (2, 16))),
        "charges": touch_ends(jax.random.randint(splits[2], (SLOTS, 3, NBLK), 0, QMOD), jax.random.fold_in(splits[2], 1), 0, QMOD - 1).astype(jnp.int32),
        "assign": touch_ends(jax.random.randint(splits[3], (SLOTS, OPS), 0, 3), jax.random.fold_in(splits[3], 1), 0, 2).astype(jnp.int32),
    }


def block_mask(charge_row):
    spread = jnp.repeat(charge_row, BLOCK, axis=1)
    charge_sum = spread[0][:, None, None] + spread[1][None, :, None] - spread[2][None, None, :]
    return jnp.mod(charge_sum, QMOD) == 0


def renormalize(weight, left_ops, right_ops, take_left, take_right):
    weight_wide = weight.astype(jnp.float32)
    left_mixed = jnp.einsum('kca,abq->kcbq', left_ops.astype(jnp.float32), weight_wide).astype(jnp.bfloat16)
    left_part = jnp.einsum('cbp,kcbq->kpq', weight_wide, left_mixed.astype(jnp.float32))
    right_mixed = jnp.einsum('kcb,abq->kacq', right_ops.astype(jnp.float32), weight_wide).astype(jnp.bfloat16)
    right_part = jnp.einsum('acp,kacq->kpq', weight_wide, right_mixed.astype(jnp.float32))
    combined = take_left[:, None, None] * left_part + take_right[:, None, None] * right_part
    return combined.astype(jnp.bfloat16)


def one_slot(packed):
    weight_raw, charge_row, assign_row, left_ops, right_ops = packed
    weight = jnp.where(block_mask(charge_row), weight_raw, jnp.zeros((), weight_raw.dtype))
    take_left = (assign_row != 1).astype(jnp.float32)
    take_right = (assign_row != 0).astype(jnp.float32)
    return renormalize(weight, left_ops, right_ops, take_left, take_right)


def reference(isometries, leaf_ops, charges, assign):
    held = leaf_ops.astype(jnp.bfloat16)
    for level_now in range(1, LEVELS + 1):
        reach_by = 2 ** (level_now - 1)
        left_all = jnp.roll(held, reach_by, axis=0)
        held = lax.map(one_slot, (isometries, charges, assign, left_all, held))
    return held
```

```python
import functools

import jax
import jax.numpy as jnp
from jax import lax
from jax.experimental import pallas as pl
from jax.experimental.pallas import tpu as pltpu
from jax.sharding import PartitionSpec as P

NBLK = 4
LEVELS = 3
CHUNKS = 4
BF = jnp.bfloat16
F32 = jnp.float32
MESH = pl.DeviceIdType.MESH


def dot(a, b):
    return jnp.dot(a, b, preferred_element_type=F32)


def kernel(
    n, leaves, iso, leaf_op, charges, assign, out,
    mm, sendb, mb, vt, ut, mask, perm, scaled, acc, xs, rbuf, lbuf, zbuf, rss, rsr,
    load_sem, a2a_send, a2a_recv, r_send, r_recv, l_send, l_recv, z_send, z_recv, s_send, s_recv,
):
    slab, chi, _ = iso.shape
    block = chi // NBLK
    per = slab // CHUNKS
    me = lax.axis_index("bond")
    slot = lax.axis_index("leaf")

    def peer(off):
        return lax.rem(me + off, n)

    def ahead(by):
        return lax.rem(slot + by, leaves)

    def rows(i):
        return pl.ds(pl.multiple_of(i * slab, slab), slab)

    mine = rows(me)

    load = pltpu.make_async_copy(iso, mm, load_sem)
    load.start()

    barrier = pltpu.get_barrier_semaphore()

    def greet(off, carry):
        pl.semaphore_signal(barrier, inc=1, device_id=(slot, peer(off)), device_id_type=MESH)
        return carry

    lax.fori_loop(1, n, greet, 0)
    for level in range(LEVELS):
        for by in (2**level, leaves - 2**level):
            pl.semaphore_signal(barrier, inc=1, device_id=(ahead(by), me), device_id_type=MESH)

    row_block = lax.broadcasted_iota(jnp.int32, (chi, chi), 0) // block
    col_block = lax.broadcasted_iota(jnp.int32, (chi, chi), 1) // block
    total = jnp.zeros((chi, chi), jnp.int32) + charges[0, (me * slab) // block]
    for k in range(NBLK):
        total = total + jnp.where(row_block == k, charges[1, k], 0) - jnp.where(col_block == k, charges[2, k], 0)
    mask[...] = jnp.where((total & 3) == 0, 1.0, 0.0).astype(BF)

    side = slab * slab
    to = lax.broadcasted_iota(jnp.int32, (side, side), 0)
    frm = lax.broadcasted_iota(jnp.int32, (side, side), 1)
    perm[...] = jnp.where((to // slab == frm % slab) & (to % slab == frm // slab), 1.0, 0.0).astype(BF)

    load.wait()

    def prepare(e, carry):
        piece = mm[:, rows(e), :] * mask[rows(e), :][None]
        mm[:, rows(e), :] = piece
        turned = dot(perm[...], piece.reshape(side, chi)).astype(BF)
        sendb[e] = turned.reshape(slab, slab, chi)
        return carry

    lax.fori_loop(0, n, prepare, 0)
    mb[:, mine, :] = sendb[me]

    pl.semaphore_wait(barrier, n - 1 + 2 * LEVELS)

    def spread(src, dst, level, send, recv):
        def go(off, carry):
            pltpu.make_async_remote_copy(
                src_ref=src, dst_ref=dst.at[level, mine], send_sem=send.at[level], recv_sem=recv.at[level],
                device_id=(slot, peer(off)), device_id_type=MESH,
            ).start()
            return carry

        lax.fori_loop(1, n, go, 0)

    def drain(ref, sem):
        pltpu.make_async_copy(ref, ref, sem).wait()

    others = pl.ds(0, chi - slab)

    def hand_on(src, level):
        return pltpu.make_async_remote_copy(
            src_ref=src, dst_ref=zbuf.at[level], send_sem=z_send.at[level], recv_sem=z_recv.at[level],
            device_id=(ahead(2**level), me), device_id_type=MESH,
        )

    def publish(src, level):
        hand_on(src, level).start()
        rbuf[level, mine] = src[...]
        spread(src, rbuf, level, r_send, r_recv)

    def forward(src, level):
        hand_on(src, level).wait_recv()
        lbuf[level, mine] = zbuf[level]
        spread(zbuf.at[level], lbuf, level, l_send, l_recv)

    def exchange(c):
        part = pl.ds(c * per, per)

        def go(off, carry):
            to_dev = peer(off)
            pltpu.make_async_remote_copy(
                src_ref=sendb.at[to_dev, part], dst_ref=mb.at[part, mine],
                send_sem=a2a_send.at[c], recv_sem=a2a_recv.at[c],
                device_id=(slot, to_dev), device_id_type=MESH,
            ).start()
            return carry

        lax.fori_loop(1, n, go, 0)

    publish(leaf_op, 0)
    exchange(0)
    forward(leaf_op, 0)
    for c in range(1, CHUNKS):
        exchange(c)

    def flip(a, carry):
        vt[a] = mm[a].T
        return carry

    lax.fori_loop(0, slab, flip, 0)

    take_left = jnp.where(assign[0] != 1, 1.0, 0.0).astype(BF)
    take_right = jnp.where(assign[0] != 0, 1.0, 0.0).astype(BF)

    def contract(turned, plain, first, count):
        def step(i, carry):
            mixed = dot(turned[i], scaled[...]).astype(BF)
            acc[...] += dot(mixed, plain[i])
            return carry

        lax.fori_loop(first, first + count, step, 0)

    for level in range(LEVELS):
        drain(rbuf.at[level, others], r_recv.at[level])
        scaled[...] = rbuf[level] * take_right
        acc[...] = jnp.zeros_like(acc)
        if level > 0:
            forward(xs.at[level - 1], level)
        contract(vt, mm, 0, slab)
        drain(lbuf.at[level, others], l_recv.at[level])
        scaled[...] = lbuf[level] * take_left
        if level == 0:
            for c in range(CHUNKS):
                drain(mb.at[pl.ds(c * per, per), others], a2a_recv.at[c])

                def turn(b, carry):
                    ut[b] = mb[b].T
                    return carry

                lax.fori_loop(c * per, (c + 1) * per, turn, 0)
                contract(ut, mb, c * per, per)
        else:
            contract(ut, mb, 0, slab)

        rss[level] = acc[...].astype(BF)
        rsr[level, me] = rss[level, mine]

        def scatter(off, carry):
            to_dev = peer(off)
            pltpu.make_async_remote_copy(
                src_ref=rss.at[level, rows(to_dev)], dst_ref=rsr.at[level, me],
                send_sem=s_send.at[level], recv_sem=s_recv.at[level],
                device_id=(slot, to_dev), device_id_type=MESH,
            ).start()
            return carry

        lax.fori_loop(1, n, scatter, 0)
        drain(rsr.at[level, pl.ds(0, n - 1)], s_recv.at[level])
        whole = rsr[level, 0].astype(F32)
        for i in range(1, n):
            whole = whole + rsr[level, i].astype(F32)
        if level < LEVELS - 1:
            xs[level] = whole.astype(BF)
            publish(xs.at[level], level + 1)
        else:
            out[...] = whole.astype(BF)

    for c in range(CHUNKS):
        drain(mb.at[pl.ds(c * per, per), others], a2a_send.at[c])
    for level in range(LEVELS):
        drain(rbuf.at[level, others], r_send.at[level])
        drain(lbuf.at[level, others], l_send.at[level])
        drain(zbuf.at[level], z_send.at[level])
        drain(rsr.at[level, pl.ds(0, n - 1)], s_send.at[level])


def shards(isometries, leaf_ops, charges, assign):
    iso = isometries[0]
    slab, chi, _ = iso.shape
    n = lax.axis_size("bond")
    leaves = lax.axis_size("leaf")
    sem = pltpu.SemaphoreType.DMA
    result = pl.pallas_call(
        functools.partial(kernel, n, leaves),
        out_shape=jax.ShapeDtypeStruct((slab, chi), BF),
        in_specs=[
            pl.BlockSpec(memory_space=pl.ANY),
            pl.BlockSpec(memory_space=pltpu.VMEM),
            pl.BlockSpec(memory_space=pltpu.SMEM),
            pl.BlockSpec(memory_space=pltpu.SMEM),
        ],
        out_specs=pl.BlockSpec(memory_space=pltpu.VMEM),
        scratch_shapes=[
            pltpu.VMEM((slab, chi, chi), BF),
            pltpu.VMEM((n, slab, slab, chi), BF),
            pltpu.VMEM((slab, chi, chi), BF),
            pltpu.VMEM((slab, chi, chi), BF),
            pltpu.VMEM((slab, chi, chi), BF),
            pltpu.VMEM((chi, chi), BF),
            pltpu.VMEM((slab * slab, slab * slab), BF),
            pltpu.VMEM((chi, chi), BF),
            pltpu.VMEM((chi, chi), F32),
            pltpu.VMEM((LEVELS, slab, chi), BF),
            pltpu.VMEM((LEVELS, chi, chi), BF),
            pltpu.VMEM((LEVELS, chi, chi), BF),
            pltpu.VMEM((LEVELS, slab, chi), BF),
            pltpu.VMEM((LEVELS, chi, chi), BF),
            pltpu.VMEM((LEVELS, n, slab, chi), BF),
            sem,
            sem((CHUNKS,)), sem((CHUNKS,)),
            sem((LEVELS,)), sem((LEVELS,)),
            sem((LEVELS,)), sem((LEVELS,)),
            sem((LEVELS,)), sem((LEVELS,)),
            sem((LEVELS,)), sem((LEVELS,)),
        ],
        compiler_params=pltpu.CompilerParams(collective_id=0, has_side_effects=True),
    )(iso, leaf_ops[0, 0], charges[0], assign[0])
    return result[None, None]


def solution(mesh):
    in_specs = (
        P("leaf", "bond", None, None),
        P("leaf", None, "bond", None),
        P("leaf", None, None),
        P("leaf", None),
    )
    out_specs = P("leaf", None, "bond", None)
    return jax.shard_map(shards, mesh=mesh, in_specs=in_specs, out_specs=out_specs, check_vma=False)
```

```python
import functools

import jax
import jax.numpy as jnp
from jax import lax
from jax.experimental import pallas as pl
from jax.experimental.pallas import tpu as pltpu
from jax.sharding import PartitionSpec as P

NBLK = 4
LEVELS = 3
CHUNKS = 4
BF = jnp.bfloat16
F32 = jnp.float32
MESH = pl.DeviceIdType.MESH


def dot(a, b):
    return jnp.dot(a, b, preferred_element_type=F32)


def kernel(
    n, leaves, iso, leaf_op, charges, assign, out,
    mm, sendb, mb, vt, ut, mask, perm, scaled, acc, xs, rbuf, lbuf, zbuf, rss, rsr,
    load_sem, a2a_send, a2a_recv, r_send, r_recv, l_send, l_recv, z_send, z_recv, s_send, s_recv,
):
    slab, chi, _ = iso.shape
    block = chi // NBLK
    per = slab // CHUNKS
    me = lax.axis_index("bond")
    slot = lax.axis_index("leaf")

    def peer(off):
        return lax.rem(me + off, n)

    def ahead(by):
        return lax.rem(slot + by, leaves)

    def rows(i):
        return pl.ds(pl.multiple_of(i * slab, slab), slab)

    mine = rows(me)

    load = pltpu.make_async_copy(iso, mm, load_sem)
    load.start()

    barrier = pltpu.get_barrier_semaphore()

    def greet(off, carry):
        pl.semaphore_signal(barrier, inc=1, device_id=(slot, peer(off)), device_id_type=MESH)
        return carry

    lax.fori_loop(1, n, greet, 0)
    for level in range(LEVELS):
        pl.semaphore_signal(barrier, inc=1, device_id=(ahead(leaves - 2**level), me), device_id_type=MESH)

    row_block = lax.broadcasted_iota(jnp.int32, (chi, chi), 0) // block
    col_block = lax.broadcasted_iota(jnp.int32, (chi, chi), 1) // block
    total = jnp.zeros((chi, chi), jnp.int32) + charges[0, 0, (me * slab) // block]
    for k in range(NBLK):
        total = total + jnp.where(row_block == k, charges[1, 0, k], 0) - jnp.where(col_block == k, charges[2, 0, k], 0)
    mask[...] = jnp.where((total & 3) == 0, 1.0, 0.0).astype(BF)

    side = slab * slab
    to = lax.broadcasted_iota(jnp.int32, (side, side), 0)
    frm = lax.broadcasted_iota(jnp.int32, (side, side), 1)
    perm[...] = jnp.where((to // slab == frm % slab) & (to % slab == frm // slab), 1.0, 0.0).astype(BF)

    load.wait()

    def prepare(e, carry):
        piece = mm[:, rows(e), :] * mask[rows(e), :][None]
        mm[:, rows(e), :] = piece
        turned = dot(perm[...], piece.reshape(side, chi)).astype(BF)
        sendb[e] = turned.reshape(slab, slab, chi)
        return carry

    lax.fori_loop(0, n, prepare, 0, unroll=4)
    mb[:, mine, :] = sendb[me]

    pl.semaphore_wait(barrier, n - 1 + LEVELS)

    def spread(src, dst, level, send, recv):
        def go(off, carry):
            pltpu.make_async_remote_copy(
                src_ref=src, dst_ref=dst.at[level, mine], send_sem=send.at[level], recv_sem=recv.at[level],
                device_id=(slot, peer(off)), device_id_type=MESH,
            ).start()
            return carry

        lax.fori_loop(1, n, go, 0)

    def drain(ref, sem):
        pltpu.make_async_copy(ref, ref, sem).wait()

    others = pl.ds(0, chi - slab)

    def hand_on(src, level):
        return pltpu.make_async_remote_copy(
            src_ref=src, dst_ref=zbuf.at[level], send_sem=z_send.at[level], recv_sem=z_recv.at[level],
            device_id=(ahead(2**level), me), device_id_type=MESH,
        )

    def publish(src, level):
        hand_on(src, level).start()
        rbuf[level, mine] = src[...]
        spread(src, rbuf, level, r_send, r_recv)

    def forward(src, level):
        hand_on(src, level).wait_recv()
        lbuf[level, mine] = zbuf[level]
        spread(zbuf.at[level], lbuf, level, l_send, l_recv)

    def exchange(c):
        part = pl.ds(c * per, per)

        def go(off, carry):
            to_dev = peer(off)
            pltpu.make_async_remote_copy(
                src_ref=sendb.at[to_dev, part], dst_ref=mb.at[part, mine],
                send_sem=a2a_send.at[c], recv_sem=a2a_recv.at[c],
                device_id=(slot, to_dev), device_id_type=MESH,
            ).start()
            return carry

        lax.fori_loop(1, n, go, 0)

    publish(leaf_op, 0)
    exchange(0)
    forward(leaf_op, 0)
    for c in range(1, CHUNKS):
        exchange(c)

    def flip(a, carry):
        vt[a] = mm[a].T
        return carry

    lax.fori_loop(0, slab, flip, 0, unroll=4)

    take_left = jnp.where(assign[0] != 1, 1.0, 0.0).astype(BF)
    take_right = jnp.where(assign[0] != 0, 1.0, 0.0).astype(BF)

    def contract(turned, plain, first, count):
        def step(i, carry):
            mixed = dot(turned[i], scaled[...]).astype(BF)
            acc[...] += dot(mixed, plain[i])
            return carry

        lax.fori_loop(first, first + count, step, 0, unroll=True)

    for level in range(LEVELS):
        if level > 0:
            forward(xs.at[level - 1], level)
        drain(rbuf.at[level, others], r_recv.at[level])
        scaled[...] = rbuf[level] * take_right
        acc[...] = jnp.zeros_like(acc)
        contract(vt, mm, 0, slab)
        drain(lbuf.at[level, others], l_recv.at[level])
        scaled[...] = lbuf[level] * take_left
        if level == 0:
            for c in range(CHUNKS):
                drain(mb.at[pl.ds(c * per, per), others], a2a_recv.at[c])

                def turn(b, carry):
                    ut[b] = mb[b].T
                    return carry

                lax.fori_loop(c * per, (c + 1) * per, turn, 0, unroll=True)
                contract(ut, mb, c * per, per)
        else:
            contract(ut, mb, 0, slab)

        rss[level] = acc[...].astype(BF)
        rsr[level, me] = rss[level, mine]

        def scatter(off, carry):
            to_dev = peer(off)
            pltpu.make_async_remote_copy(
                src_ref=rss.at[level, rows(to_dev)], dst_ref=rsr.at[level, me],
                send_sem=s_send.at[level], recv_sem=s_recv.at[level],
                device_id=(slot, to_dev), device_id_type=MESH,
            ).start()
            return carry

        lax.fori_loop(1, n, scatter, 0)
        drain(rsr.at[level, pl.ds(0, n - 1)], s_recv.at[level])
        whole = rsr[level, 0].astype(F32)
        for i in range(1, n):
            whole = whole + rsr[level, i].astype(F32)
        if level < LEVELS - 1:
            xs[level] = whole.astype(BF)
            publish(xs.at[level], level + 1)
        else:
            out[...] = whole.astype(BF)

    for c in range(CHUNKS):
        drain(mb.at[pl.ds(c * per, per), others], a2a_send.at[c])
    for level in range(LEVELS):
        drain(rbuf.at[level, others], r_send.at[level])
        drain(lbuf.at[level, others], l_send.at[level])
        drain(zbuf.at[level], z_send.at[level])
        drain(rsr.at[level, pl.ds(0, n - 1)], s_send.at[level])


def shards(isometries, leaf_ops, charges, assign):
    iso = isometries[0]
    slab, chi, _ = iso.shape
    n = lax.axis_size("bond")
    leaves = lax.axis_size("leaf")
    sem = pltpu.SemaphoreType.DMA
    result = pl.pallas_call(
        functools.partial(kernel, n, leaves),
        out_shape=jax.ShapeDtypeStruct((slab, chi), BF),
        in_specs=[
            pl.BlockSpec(memory_space=pl.ANY),
            pl.BlockSpec(memory_space=pltpu.VMEM),
            pl.BlockSpec(memory_space=pltpu.SMEM),
            pl.BlockSpec(memory_space=pltpu.SMEM),
        ],
        out_specs=pl.BlockSpec(memory_space=pltpu.VMEM),
        scratch_shapes=[
            pltpu.VMEM((slab, chi, chi), BF),
            pltpu.VMEM((n, slab, slab, chi), BF),
            pltpu.VMEM((slab, chi, chi), BF),
            pltpu.VMEM((slab, chi, chi), BF),
            pltpu.VMEM((slab, chi, chi), BF),
            pltpu.VMEM((chi, chi), BF),
            pltpu.VMEM((slab * slab, slab * slab), BF),
            pltpu.VMEM((chi, chi), BF),
            pltpu.VMEM((chi, chi), F32),
            pltpu.VMEM((LEVELS, slab, chi), BF),
            pltpu.VMEM((LEVELS, chi, chi), BF),
            pltpu.VMEM((LEVELS, chi, chi), BF),
            pltpu.VMEM((LEVELS, slab, chi), BF),
            pltpu.VMEM((LEVELS, chi, chi), BF),
            pltpu.VMEM((LEVELS, n, slab, chi), BF),
            sem,
            sem((CHUNKS,)), sem((CHUNKS,)),
            sem((LEVELS,)), sem((LEVELS,)),
            sem((LEVELS,)), sem((LEVELS,)),
            sem((LEVELS,)), sem((LEVELS,)),
            sem((LEVELS,)), sem((LEVELS,)),
        ],
        compiler_params=pltpu.CompilerParams(collective_id=0, has_side_effects=True),
    )(iso, leaf_ops[0, 0], jnp.transpose(charges, (1, 0, 2)), assign[0])
    return result[None, None]


def solution(mesh):
    in_specs = (
        P("leaf", "bond", None, None),
        P("leaf", None, "bond", None),
        P("leaf", None, None),
        P("leaf", None),
    )
    out_specs = P("leaf", None, "bond", None)
    return jax.shard_map(shards, mesh=mesh, in_specs=in_specs, out_specs=out_specs, check_vma=False)
```

```python
import functools
import math

import jax
import jax.numpy as jnp
from jax import lax
from jax.experimental import pallas as pl
from jax.experimental.pallas import tpu as pltpu
from jax.sharding import PartitionSpec as P

NBLK = 4
LEVELS = 3
CHUNKS = 4
BF = jnp.bfloat16
F32 = jnp.float32
MESH = pl.DeviceIdType.MESH


def dot(a, b):
    return jnp.dot(a, b, preferred_element_type=F32)


def kernel(
    n, leaves, iso, leaf_op, charges, assign, out,
    mm, sendb, mb, vt, ut, mask, perm, scaled, acc, xs, rbuf, lbuf, zbuf, rss, rsr,
    load_sem, a2a_send, a2a_recv, r_send, r_recv, l_send, l_recv, z_send, z_recv, s_send, s_recv,
):
    slab, chi, _ = iso.shape
    block = chi // NBLK
    per = slab // CHUNKS
    me = lax.axis_index("bond")
    slot = lax.axis_index("leaf")

    width = math.isqrt(n)
    steps = sorted(
        ((i, j) for i in range(width) for j in range(width)),
        key=lambda at: -sum(min(k, width - k) for k in at),
    )
    others_at = steps[:-1]

    def peer(at):
        return lax.rem(me // width + at[0], width) * width + lax.rem(lax.rem(me, width) + at[1], width)

    def ahead(by):
        return lax.rem(slot + by, leaves)

    def rows(i):
        return pl.ds(pl.multiple_of(i * slab, slab), slab)

    mine = rows(me)

    load = pltpu.make_async_copy(iso, mm, load_sem)
    load.start()

    barrier = pltpu.get_barrier_semaphore()

    for at in others_at:
        pl.semaphore_signal(barrier, inc=1, device_id=(slot, peer(at)), device_id_type=MESH)
    pl.semaphore_signal(barrier, inc=1, device_id=(ahead(leaves - 1), me), device_id_type=MESH)
    for level in range(1, LEVELS):
        for at in steps:
            pl.semaphore_signal(
                barrier, inc=1, device_id=(ahead(leaves - 2**level), peer(at)), device_id_type=MESH
            )

    row_block = lax.broadcasted_iota(jnp.int32, (chi, chi), 0) // block
    col_block = lax.broadcasted_iota(jnp.int32, (chi, chi), 1) // block
    total = jnp.zeros((chi, chi), jnp.int32) + charges[0, 0, (me * slab) // block]
    for k in range(NBLK):
        total = total + jnp.where(row_block == k, charges[1, 0, k], 0) - jnp.where(col_block == k, charges[2, 0, k], 0)
    mask[...] = jnp.where((total & 3) == 0, 1.0, 0.0).astype(BF)

    side = slab * slab
    to = lax.broadcasted_iota(jnp.int32, (side, side), 0)
    frm = lax.broadcasted_iota(jnp.int32, (side, side), 1)
    perm[...] = jnp.where((to // slab == frm % slab) & (to % slab == frm // slab), 1.0, 0.0).astype(BF)

    load.wait()

    def prepare(e, carry):
        piece = mm[:, rows(e), :] * mask[rows(e), :][None]
        mm[:, rows(e), :] = piece
        turned = dot(perm[...], piece.reshape(side, chi)).astype(BF)
        sendb[e] = turned.reshape(slab, slab, chi)
        return carry

    lax.fori_loop(0, n, prepare, 0, unroll=4)
    mb[:, mine, :] = sendb[me]

    pl.semaphore_wait(barrier, n + n * (LEVELS - 1))

    def post(src, dst, level, send, recv, to_slot, at):
        pltpu.make_async_remote_copy(
            src_ref=src, dst_ref=dst.at[level, mine], send_sem=send.at[level], recv_sem=recv.at[level],
            device_id=(to_slot, peer(at)), device_id_type=MESH,
        ).start()

    def drain(ref, sem):
        pltpu.make_async_copy(ref, ref, sem).wait()

    others = pl.ds(0, chi - slab)

    hand_on = pltpu.make_async_remote_copy(
        src_ref=leaf_op, dst_ref=zbuf, send_sem=z_send, recv_sem=z_recv,
        device_id=(ahead(1), me), device_id_type=MESH,
    )

    def publish(src, level):
        for at in steps:
            if level > 0:
                post(src, lbuf, level, l_send, l_recv, ahead(2**level), at)
            if at != (0, 0):
                post(src, rbuf, level, r_send, r_recv, slot, at)
        rbuf[level, mine] = src[...]

    def exchange(c):
        part = pl.ds(c * per, per)

        for at in others_at:
            to_dev = peer(at)
            pltpu.make_async_remote_copy(
                src_ref=sendb.at[to_dev, part], dst_ref=mb.at[part, mine],
                send_sem=a2a_send.at[c], recv_sem=a2a_recv.at[c],
                device_id=(slot, to_dev), device_id_type=MESH,
            ).start()

    hand_on.start()
    publish(leaf_op, 0)
    exchange(0)
    hand_on.wait_recv()
    lbuf[0, mine] = zbuf[...]
    for at in others_at:
        post(zbuf, lbuf, 0, l_send, l_recv, slot, at)
    for c in range(1, CHUNKS):
        exchange(c)

    def flip(a, carry):
        vt[a] = mm[a].T
        return carry

    lax.fori_loop(0, slab, flip, 0, unroll=4)

    take_left = jnp.where(assign[0] != 1, 1.0, 0.0).astype(BF)
    take_right = jnp.where(assign[0] != 0, 1.0, 0.0).astype(BF)

    def contract(turned, plain, first, count):
        def step(i, carry):
            mixed = dot(turned[i], scaled[...]).astype(BF)
            acc[...] += dot(mixed, plain[i])
            return carry

        lax.fori_loop(first, first + count, step, 0, unroll=True)

    for level in range(LEVELS):
        drain(rbuf.at[level, others], r_recv.at[level])
        scaled[...] = rbuf[level] * take_right
        acc[...] = jnp.zeros_like(acc)
        contract(vt, mm, 0, slab)
        drain(lbuf.at[level] if level > 0 else lbuf.at[level, others], l_recv.at[level])
        scaled[...] = lbuf[level] * take_left
        if level == 0:
            for c in range(CHUNKS):
                drain(mb.at[pl.ds(c * per, per), others], a2a_recv.at[c])

                def turn(b, carry):
                    ut[b] = mb[b].T
                    return carry

                lax.fori_loop(c * per, (c + 1) * per, turn, 0, unroll=True)
                contract(ut, mb, c * per, per)
        else:
            contract(ut, mb, 0, slab)

        rss[level] = acc[...].astype(BF)
        for at in others_at:
            to_dev = peer(at)
            pltpu.make_async_remote_copy(
                src_ref=rss.at[level, rows(to_dev)], dst_ref=rsr.at[level, me],
                send_sem=s_send.at[level], recv_sem=s_recv.at[level],
                device_id=(slot, to_dev), device_id_type=MESH,
            ).start()
        rsr[level, me] = rss[level, mine]
        drain(rsr.at[level, pl.ds(0, n - 1)], s_recv.at[level])
        whole = rsr[level, 0].astype(F32)
        for i in range(1, n):
            whole = whole + rsr[level, i].astype(F32)
        if level < LEVELS - 1:
            xs[level] = whole.astype(BF)
            publish(xs.at[level], level + 1)
        else:
            out[...] = whole.astype(BF)

    hand_on.wait_send()
    for c in range(CHUNKS):
        drain(mb.at[pl.ds(c * per, per), others], a2a_send.at[c])
    for level in range(LEVELS):
        drain(rbuf.at[level, others], r_send.at[level])
        drain(lbuf.at[level] if level > 0 else lbuf.at[level, others], l_send.at[level])
        drain(rsr.at[level, pl.ds(0, n - 1)], s_send.at[level])


def shards(isometries, leaf_ops, charges, assign):
    iso = isometries[0]
    slab, chi, _ = iso.shape
    n = lax.axis_size("bond")
    leaves = lax.axis_size("leaf")
    sem = pltpu.SemaphoreType.DMA
    result = pl.pallas_call(
        functools.partial(kernel, n, leaves),
        out_shape=jax.ShapeDtypeStruct((slab, chi), BF),
        in_specs=[
            pl.BlockSpec(memory_space=pl.ANY),
            pl.BlockSpec(memory_space=pltpu.VMEM),
            pl.BlockSpec(memory_space=pltpu.SMEM),
            pl.BlockSpec(memory_space=pltpu.SMEM),
        ],
        out_specs=pl.BlockSpec(memory_space=pltpu.VMEM),
        scratch_shapes=[
            pltpu.VMEM((slab, chi, chi), BF),
            pltpu.VMEM((n, slab, slab, chi), BF),
            pltpu.VMEM((slab, chi, chi), BF),
            pltpu.VMEM((slab, chi, chi), BF),
            pltpu.VMEM((slab, chi, chi), BF),
            pltpu.VMEM((chi, chi), BF),
            pltpu.VMEM((slab * slab, slab * slab), BF),
            pltpu.VMEM((chi, chi), BF),
            pltpu.VMEM((chi, chi), F32),
            pltpu.VMEM((LEVELS, slab, chi), BF),
            pltpu.VMEM((LEVELS, chi, chi), BF),
            pltpu.VMEM((LEVELS, chi, chi), BF),
            pltpu.VMEM((slab, chi), BF),
            pltpu.VMEM((LEVELS, chi, chi), BF),
            pltpu.VMEM((LEVELS, n, slab, chi), BF),
            sem,
            sem((CHUNKS,)), sem((CHUNKS,)),
            sem((LEVELS,)), sem((LEVELS,)),
            sem((LEVELS,)), sem((LEVELS,)),
            sem, sem,
            sem((LEVELS,)), sem((LEVELS,)),
        ],
        compiler_params=pltpu.CompilerParams(collective_id=0, has_side_effects=True),
    )(iso, leaf_ops[0, 0], jnp.transpose(charges, (1, 0, 2)), assign[0])
    return result[None, None]


def solution(mesh):
    in_specs = (
        P("leaf", "bond", None, None),
        P("leaf", None, "bond", None),
        P("leaf", None, None),
        P("leaf", None),
    )
    out_specs = P("leaf", None, "bond", None)
    return jax.shard_map(shards, mesh=mesh, in_specs=in_specs, out_specs=out_specs, check_vma=False)
```

```python
import functools
import math

import jax
import jax.numpy as jnp
from jax import lax
from jax.experimental import pallas as pl
from jax.experimental.pallas import tpu as pltpu
from jax.sharding import PartitionSpec as P

NBLK = 4
LEVELS = 3
CHUNKS = 4
BF = jnp.bfloat16
F32 = jnp.float32
MESH = pl.DeviceIdType.MESH


def dot(a, b):
    return jnp.dot(a, b, preferred_element_type=F32)


def kernel(
    n, leaves, iso, leaf_hbm, charges, assign, out,
    leaf_op, mm, sendb, mb, vt, ut, mask, perm, scaled, acc, xs, rbuf, lbuf, zbuf, rss, rsr,
    load_sem, leaf_sem, a2a_send, a2a_recv, r_send, r_recv, l_send, l_recv, z_send, z_recv, s_send, s_recv,
):
    slab, chi, _ = iso.shape
    block = chi // NBLK
    per = slab // CHUNKS
    me = lax.axis_index("bond")
    slot = lax.axis_index("leaf")

    width = math.isqrt(n)
    steps = sorted(
        ((i, j) for i in range(width) for j in range(width)),
        key=lambda at: -sum(min(k, width - k) for k in at),
    )
    others_at = steps[:-1]

    def peer(at):
        return lax.rem(me // width + at[0], width) * width + lax.rem(lax.rem(me, width) + at[1], width)

    def ahead(by):
        return lax.rem(slot + by, leaves)

    def rows(i):
        return pl.ds(pl.multiple_of(i * slab, slab), slab)

    mine = rows(me)

    load = pltpu.make_async_copy(iso, mm, load_sem)
    load.start()
    load_leaf = pltpu.make_async_copy(leaf_hbm, leaf_op, leaf_sem)
    load_leaf.start()

    barrier = pltpu.get_barrier_semaphore()

    for at in others_at:
        pl.semaphore_signal(barrier, inc=1, device_id=(slot, peer(at)), device_id_type=MESH)
    pl.semaphore_signal(barrier, inc=1, device_id=(ahead(leaves - 1), me), device_id_type=MESH)
    for level in range(1, LEVELS):
        for at in steps:
            pl.semaphore_signal(
                barrier, inc=1, device_id=(ahead(leaves - 2**level), peer(at)), device_id_type=MESH
            )

    row_block = lax.broadcasted_iota(jnp.int32, (chi, chi), 0) // block
    col_block = lax.broadcasted_iota(jnp.int32, (chi, chi), 1) // block
    total = jnp.zeros((chi, chi), jnp.int32) + charges[0, 0, (me * slab) // block]
    for k in range(NBLK):
        total = total + jnp.where(row_block == k, charges[1, 0, k], 0) - jnp.where(col_block == k, charges[2, 0, k], 0)
    mask[...] = jnp.where((total & 3) == 0, 1.0, 0.0).astype(BF)

    side = slab * slab
    to = lax.broadcasted_iota(jnp.int32, (side, side), 0)
    frm = lax.broadcasted_iota(jnp.int32, (side, side), 1)
    perm[...] = jnp.where((to // slab == frm % slab) & (to % slab == frm // slab), 1.0, 0.0).astype(BF)

    load.wait()
    load_leaf.wait()

    def prepare(e, carry):
        piece = mm[:, rows(e), :] * mask[rows(e), :][None]
        mm[:, rows(e), :] = piece
        turned = dot(perm[...], piece.reshape(side, chi)).astype(BF)
        sendb[e] = turned.reshape(slab, slab, chi)
        return carry

    lax.fori_loop(0, n, prepare, 0, unroll=4)
    mb[:, mine, :] = sendb[me]

    pl.semaphore_wait(barrier, n + n * (LEVELS - 1))

    def post(src, dst, level, send, recv, to_slot, at):
        pltpu.make_async_remote_copy(
            src_ref=src, dst_ref=dst.at[level, mine], send_sem=send.at[level], recv_sem=recv.at[level],
            device_id=(to_slot, peer(at)), device_id_type=MESH,
        ).start()

    def drain(ref, sem):
        pltpu.make_async_copy(ref, ref, sem).wait()

    others = pl.ds(0, chi - slab)

    hand_on = pltpu.make_async_remote_copy(
        src_ref=leaf_op, dst_ref=zbuf, send_sem=z_send, recv_sem=z_recv,
        device_id=(ahead(1), me), device_id_type=MESH,
    )

    def publish(src, level):
        for at in steps:
            if level > 0:
                post(src, lbuf, level, l_send, l_recv, ahead(2**level), at)
            if at != (0, 0):
                post(src, rbuf, level, r_send, r_recv, slot, at)
        rbuf[level, mine] = src[...]

    def exchange(c):
        part = pl.ds(c * per, per)

        for at in reversed(others_at):
            to_dev = peer(at)
            pltpu.make_async_remote_copy(
                src_ref=sendb.at[to_dev, part], dst_ref=mb.at[part, mine],
                send_sem=a2a_send.at[c], recv_sem=a2a_recv.at[c],
                device_id=(slot, to_dev), device_id_type=MESH,
            ).start()

    def flip(a, carry):
        vt[a] = mm[a].T
        return carry


    take_left = jnp.where(assign[0] != 1, 1.0, 0.0).astype(BF)
    take_right = jnp.where(assign[0] != 0, 1.0, 0.0).astype(BF)

    def contract(turned, plain, first, count):
        def step(i, carry):
            mixed = dot(turned[i], scaled[...]).astype(BF)
            acc[...] += dot(mixed, plain[i])
            return carry

        lax.fori_loop(first, first + count, step, 0, unroll=True)

    def right_part(level):
        drain(rbuf.at[level, others], r_recv.at[level])
        scaled[...] = rbuf[level] * take_right
        acc[...] = jnp.zeros_like(acc)
        contract(vt, mm, 0, slab)

    hand_on.start()
    publish(leaf_op, 0)
    exchange(0)
    exchange(1)
    lax.fori_loop(0, slab, flip, 0, unroll=4)
    hand_on.wait_recv()
    lbuf[0, mine] = zbuf[...]
    for at in others_at:
        post(zbuf, lbuf, 0, l_send, l_recv, slot, at)
    exchange(2)
    right_part(0)
    for c in range(3, CHUNKS):
        exchange(c)

    for level in range(LEVELS):
        if level > 0:
            right_part(level)
        drain(lbuf.at[level] if level > 0 else lbuf.at[level, others], l_recv.at[level])
        scaled[...] = lbuf[level] * take_left
        if level == 0:
            for c in range(CHUNKS):
                drain(mb.at[pl.ds(c * per, per), others], a2a_recv.at[c])

                def turn(b, carry):
                    ut[b] = mb[b].T
                    return carry

                lax.fori_loop(c * per, (c + 1) * per, turn, 0, unroll=True)
                contract(ut, mb, c * per, per)
        else:
            contract(ut, mb, 0, slab)

        rss[level] = acc[...].astype(BF)
        for at in others_at:
            to_dev = peer(at)
            pltpu.make_async_remote_copy(
                src_ref=rss.at[level, rows(to_dev)], dst_ref=rsr.at[level, me],
                send_sem=s_send.at[level], recv_sem=s_recv.at[level],
                device_id=(slot, to_dev), device_id_type=MESH,
            ).start()
        rsr[level, me] = rss[level, mine]
        drain(rsr.at[level, pl.ds(0, n - 1)], s_recv.at[level])
        whole = rsr[level, 0].astype(F32)
        for i in range(1, n):
            whole = whole + rsr[level, i].astype(F32)
        if level < LEVELS - 1:
            xs[level] = whole.astype(BF)
            publish(xs.at[level], level + 1)
        else:
            out[...] = whole

    hand_on.wait_send()
    for c in range(CHUNKS):
        drain(mb.at[pl.ds(c * per, per), others], a2a_send.at[c])
    for level in range(LEVELS):
        drain(rbuf.at[level, others], r_send.at[level])
        drain(lbuf.at[level] if level > 0 else lbuf.at[level, others], l_send.at[level])
        drain(rsr.at[level, pl.ds(0, n - 1)], s_send.at[level])


def shards(isometries, leaf_ops, charges, assign):
    iso = isometries[0]
    slab, chi, _ = iso.shape
    n = lax.axis_size("bond")
    leaves = lax.axis_size("leaf")
    sem = pltpu.SemaphoreType.DMA
    result = pl.pallas_call(
        functools.partial(kernel, n, leaves),
        out_shape=jax.ShapeDtypeStruct((slab, chi), F32),
        in_specs=[
            pl.BlockSpec(memory_space=pl.ANY),
            pl.BlockSpec(memory_space=pl.ANY),
            pl.BlockSpec(memory_space=pltpu.SMEM),
            pl.BlockSpec(memory_space=pltpu.SMEM),
        ],
        out_specs=pl.BlockSpec(memory_space=pltpu.VMEM),
        scratch_shapes=[
            pltpu.VMEM((slab, chi), BF),
            pltpu.VMEM((slab, chi, chi), BF),
            pltpu.VMEM((n, slab, slab, chi), BF),
            pltpu.VMEM((slab, chi, chi), BF),
            pltpu.VMEM((slab, chi, chi), BF),
            pltpu.VMEM((slab, chi, chi), BF),
            pltpu.VMEM((chi, chi), BF),
            pltpu.VMEM((slab * slab, slab * slab), BF),
            pltpu.VMEM((chi, chi), BF),
            pltpu.VMEM((chi, chi), F32),
            pltpu.VMEM((LEVELS, slab, chi), BF),
            pltpu.VMEM((LEVELS, chi, chi), BF),
            pltpu.VMEM((LEVELS, chi, chi), BF),
            pltpu.VMEM((slab, chi), BF),
            pltpu.VMEM((LEVELS, chi, chi), BF),
            pltpu.VMEM((LEVELS, n, slab, chi), BF),
            sem, sem,
            sem((CHUNKS,)), sem((CHUNKS,)),
            sem((LEVELS,)), sem((LEVELS,)),
            sem((LEVELS,)), sem((LEVELS,)),
            sem, sem,
            sem((LEVELS,)), sem((LEVELS,)),
        ],
        compiler_params=pltpu.CompilerParams(collective_id=0, has_side_effects=True),
    )(iso, leaf_ops[0, 0], jnp.transpose(charges, (1, 0, 2)), assign[0])
    return result.astype(BF)[None, None]


def solution(mesh):
    in_specs = (
        P("leaf", "bond", None, None),
        P("leaf", None, "bond", None),
        P("leaf", None, None),
        P("leaf", None),
    )
    out_specs = P("leaf", None, "bond", None)
    return jax.shard_map(shards, mesh=mesh, in_specs=in_specs, out_specs=out_specs, check_vma=False)
```

```python
import functools
import math

import jax
import jax.numpy as jnp
from jax import lax
from jax.experimental import pallas as pl
from jax.experimental.pallas import tpu as pltpu
from jax.sharding import PartitionSpec as P

NBLK = 4
LEVELS = 3
CHUNK_ROWS = (6, 5, 4, 1)
CHUNKS = len(CHUNK_ROWS)
BF = jnp.bfloat16
F32 = jnp.float32
MESH = pl.DeviceIdType.MESH


def dot(a, b):
    return jnp.dot(a, b, preferred_element_type=F32)


def kernel(
    n, leaves, iso, leaf_op, charges, assign, out,
    mm, sendb, mb, vt, ut, mask, perm, scaled, acc, xs, rbuf, lbuf, zbuf, rss, rsr,
    load_sem, a2a_send, a2a_recv, r_send, r_recv, l_send, l_recv, z_send, z_recv, s_send, s_recv,
):
    slab, chi, _ = iso.shape
    block = chi // NBLK
    starts = [sum(CHUNK_ROWS[:c]) for c in range(CHUNKS)]
    me = lax.axis_index("bond")
    slot = lax.axis_index("leaf")

    width = math.isqrt(n)
    steps = sorted(
        ((i, j) for i in range(width) for j in range(width)),
        key=lambda at: -sum(min(k, width - k) for k in at),
    )
    others_at = steps[:-1]

    def peer(at):
        return lax.rem(me // width + at[0], width) * width + lax.rem(lax.rem(me, width) + at[1], width)

    def ahead(by):
        return lax.rem(slot + by, leaves)

    def rows(i):
        return pl.ds(pl.multiple_of(i * slab, slab), slab)

    mine = rows(me)

    load = pltpu.make_async_copy(iso, mm, load_sem)
    load.start()

    barrier = pltpu.get_barrier_semaphore()

    for at in others_at:
        pl.semaphore_signal(barrier, inc=1, device_id=(slot, peer(at)), device_id_type=MESH)
    pl.semaphore_signal(barrier, inc=1, device_id=(ahead(leaves - 1), me), device_id_type=MESH)
    for level in range(1, LEVELS):
        for at in steps:
            pl.semaphore_signal(
                barrier, inc=1, device_id=(ahead(leaves - 2**level), peer(at)), device_id_type=MESH
            )

    row_block = lax.broadcasted_iota(jnp.int32, (chi, chi), 0) // block
    col_block = lax.broadcasted_iota(jnp.int32, (chi, chi), 1) // block
    total = jnp.zeros((chi, chi), jnp.int32) + charges[0, 0, (me * slab) // block]
    for k in range(NBLK):
        total = total + jnp.where(row_block == k, charges[1, 0, k], 0) - jnp.where(col_block == k, charges[2, 0, k], 0)
    mask[...] = jnp.where((total & 3) == 0, 1.0, 0.0).astype(BF)

    side = slab * slab
    to = lax.broadcasted_iota(jnp.int32, (side, side), 0)
    frm = lax.broadcasted_iota(jnp.int32, (side, side), 1)
    perm[...] = jnp.where((to // slab == frm % slab) & (to % slab == frm // slab), 1.0, 0.0).astype(BF)

    load.wait()

    def prepare(e, carry):
        piece = mm[:, rows(e), :] * mask[rows(e), :][None]
        mm[:, rows(e), :] = piece
        turned = dot(perm[...], piece.reshape(side, chi)).astype(BF)
        sendb[e] = turned.reshape(slab, slab, chi)
        return carry

    lax.fori_loop(0, n, prepare, 0, unroll=4)
    mb[:, mine, :] = sendb[me]

    pl.semaphore_wait(barrier, n + n * (LEVELS - 1))

    def post(src, dst, level, send, recv, to_slot, at):
        pltpu.make_async_remote_copy(
            src_ref=src, dst_ref=dst.at[level, mine], send_sem=send.at[level], recv_sem=recv.at[level],
            device_id=(to_slot, peer(at)), device_id_type=MESH,
        ).start()

    def drain(ref, sem):
        pltpu.make_async_copy(ref, ref, sem).wait()

    others = pl.ds(0, chi - slab)

    hand_on = pltpu.make_async_remote_copy(
        src_ref=leaf_op, dst_ref=zbuf, send_sem=z_send, recv_sem=z_recv,
        device_id=(ahead(1), me), device_id_type=MESH,
    )

    def publish(src, level):
        for at in others_at:
            post(src, rbuf, level, r_send, r_recv, slot, at)
        if level > 0:
            for at in steps:
                post(src, lbuf, level, l_send, l_recv, ahead(2**level), at)
        rbuf[level, mine] = src[...]

    def exchange(c):
        part = pl.ds(starts[c], CHUNK_ROWS[c])

        for at in others_at:
            to_dev = peer(at)
            pltpu.make_async_remote_copy(
                src_ref=sendb.at[to_dev, part], dst_ref=mb.at[part, mine],
                send_sem=a2a_send.at[c], recv_sem=a2a_recv.at[c],
                device_id=(slot, to_dev), device_id_type=MESH,
            ).start()

    hand_on.start()
    publish(leaf_op, 0)
    exchange(0)
    hand_on.wait_recv()
    lbuf[0, mine] = zbuf[...]
    for at in others_at:
        post(zbuf, lbuf, 0, l_send, l_recv, slot, at)
    for c in range(1, CHUNKS):
        exchange(c)

    def flip(a, carry):
        vt[a] = mm[a].T
        return carry

    lax.fori_loop(0, slab, flip, 0, unroll=4)

    take_left = jnp.where(assign[0] != 1, 1.0, 0.0).astype(BF)
    take_right = jnp.where(assign[0] != 0, 1.0, 0.0).astype(BF)

    def contract(turned, plain, first, count):
        def step(i, carry):
            mixed = dot(turned[i], scaled[...]).astype(BF)
            acc[...] += dot(mixed, plain[i])
            return carry

        lax.fori_loop(first, first + count, step, 0, unroll=True)

    for level in range(LEVELS):
        drain(rbuf.at[level, others], r_recv.at[level])
        scaled[...] = rbuf[level] * take_right
        acc[...] = jnp.zeros_like(acc)
        contract(vt, mm, 0, slab)
        drain(lbuf.at[level] if level > 0 else lbuf.at[level, others], l_recv.at[level])
        scaled[...] = lbuf[level] * take_left
        if level == 0:
            for c in range(CHUNKS):
                drain(mb.at[pl.ds(starts[c], CHUNK_ROWS[c]), others], a2a_recv.at[c])

                def turn(b, carry):
                    ut[b] = mb[b].T
                    return carry

                lax.fori_loop(starts[c], starts[c] + CHUNK_ROWS[c], turn, 0, unroll=True)
                contract(ut, mb, starts[c], CHUNK_ROWS[c])
        else:
            contract(ut, mb, 0, slab)

        rss[level] = acc[...].astype(BF)
        for at in others_at:
            to_dev = peer(at)
            pltpu.make_async_remote_copy(
                src_ref=rss.at[level, rows(to_dev)], dst_ref=rsr.at[level, me],
                send_sem=s_send.at[level], recv_sem=s_recv.at[level],
                device_id=(slot, to_dev), device_id_type=MESH,
            ).start()
        rsr[level, me] = rss[level, mine]
        drain(rsr.at[level, pl.ds(0, n - 1)], s_recv.at[level])
        whole = rsr[level, 0].astype(F32)
        for i in range(1, n):
            whole = whole + rsr[level, i].astype(F32)
        if level < LEVELS - 1:
            xs[level] = whole.astype(BF)
            publish(xs.at[level], level + 1)
        else:
            out[...] = whole.astype(BF)

    hand_on.wait_send()
    for c in range(CHUNKS):
        drain(mb.at[pl.ds(starts[c], CHUNK_ROWS[c]), others], a2a_send.at[c])
    for level in range(LEVELS):
        drain(rbuf.at[level, others], r_send.at[level])
        drain(lbuf.at[level] if level > 0 else lbuf.at[level, others], l_send.at[level])
        drain(rsr.at[level, pl.ds(0, n - 1)], s_send.at[level])


def shards(isometries, leaf_ops, charges, assign):
    iso = isometries[0]
    slab, chi, _ = iso.shape
    n = lax.axis_size("bond")
    leaves = lax.axis_size("leaf")
    sem = pltpu.SemaphoreType.DMA
    result = pl.pallas_call(
        functools.partial(kernel, n, leaves),
        out_shape=jax.ShapeDtypeStruct((slab, chi), BF),
        in_specs=[
            pl.BlockSpec(memory_space=pl.ANY),
            pl.BlockSpec(memory_space=pltpu.VMEM),
            pl.BlockSpec(memory_space=pltpu.SMEM),
            pl.BlockSpec(memory_space=pltpu.SMEM),
        ],
        out_specs=pl.BlockSpec(memory_space=pltpu.VMEM),
        scratch_shapes=[
            pltpu.VMEM((slab, chi, chi), BF),
            pltpu.VMEM((n, slab, slab, chi), BF),
            pltpu.VMEM((slab, chi, chi), BF),
            pltpu.VMEM((slab, chi, chi), BF),
            pltpu.VMEM((slab, chi, chi), BF),
            pltpu.VMEM((chi, chi), BF),
            pltpu.VMEM((slab * slab, slab * slab), BF),
            pltpu.VMEM((chi, chi), BF),
            pltpu.VMEM((chi, chi), F32),
            pltpu.VMEM((LEVELS, slab, chi), BF),
            pltpu.VMEM((LEVELS, chi, chi), BF),
            pltpu.VMEM((LEVELS, chi, chi), BF),
            pltpu.VMEM((slab, chi), BF),
            pltpu.VMEM((LEVELS, chi, chi), BF),
            pltpu.VMEM((LEVELS, n, slab, chi), BF),
            sem,
            sem((CHUNKS,)), sem((CHUNKS,)),
            sem((LEVELS,)), sem((LEVELS,)),
            sem((LEVELS,)), sem((LEVELS,)),
            sem, sem,
            sem((LEVELS,)), sem((LEVELS,)),
        ],
        compiler_params=pltpu.CompilerParams(collective_id=0, has_side_effects=True),
    )(iso, leaf_ops[0, 0], jnp.transpose(charges, (1, 0, 2)), assign[0])
    return result[None, None]


def solution(mesh):
    in_specs = (
        P("leaf", "bond", None, None),
        P("leaf", None, "bond", None),
        P("leaf", None, None),
        P("leaf", None),
    )
    out_specs = P("leaf", None, "bond", None)
    return jax.shard_map(shards, mesh=mesh, in_specs=in_specs, out_specs=out_specs, check_vma=False)
```

```python
import functools
import math

import jax
import jax.numpy as jnp
from jax import lax
from jax.experimental import pallas as pl
from jax.experimental.pallas import tpu as pltpu
from jax.sharding import PartitionSpec as P

NBLK = 4
LEVELS = 3
CHUNKS = 4
BF = jnp.bfloat16
F32 = jnp.float32
MESH = pl.DeviceIdType.MESH


def dot(a, b):
    return jnp.dot(a, b, preferred_element_type=F32)


def kernel(
    n, leaves, iso, leaf_op, charges, assign, out,
    mm, sendb, mb, vt, ut, mask, perm, scaled, acc, xs, rbuf, lbuf, zbuf, rss, rsr,
    load_sem, a2a_send, a2a_recv, r_send, r_recv, l_send, l_recv, z_send, z_recv, s_send, s_recv,
):
    slab, chi, _ = iso.shape
    block = chi // NBLK
    per = slab // CHUNKS
    me = lax.axis_index("bond")
    slot = lax.axis_index("leaf")

    width = math.isqrt(n)
    steps = sorted(
        ((i, j) for i in range(width) for j in range(width)),
        key=lambda at: -sum(min(k, width - k) for k in at),
    )
    others_at = steps[:-1]

    def peer(at):
        return lax.rem(me // width + at[0], width) * width + lax.rem(lax.rem(me, width) + at[1], width)

    def ahead(by):
        return lax.rem(slot + by, leaves)

    def rows(i):
        return pl.ds(pl.multiple_of(i * slab, slab), slab)

    mine = rows(me)

    load = pltpu.make_async_copy(iso, mm, load_sem)
    load.start()

    barrier = pltpu.get_barrier_semaphore()

    for at in others_at:
        pl.semaphore_signal(barrier, inc=1, device_id=(slot, peer(at)), device_id_type=MESH)
    pl.semaphore_signal(barrier, inc=1, device_id=(ahead(leaves - 1), me), device_id_type=MESH)
    for level in range(1, LEVELS):
        for at in steps:
            pl.semaphore_signal(
                barrier, inc=1, device_id=(ahead(leaves - 2**level), peer(at)), device_id_type=MESH
            )

    row_block = lax.broadcasted_iota(jnp.int32, (chi, chi), 0) // block
    col_block = lax.broadcasted_iota(jnp.int32, (chi, chi), 1) // block
    total = jnp.zeros((chi, chi), jnp.int32) + charges[0, 0, (me * slab) // block]
    for k in range(NBLK):
        total = total + jnp.where(row_block == k, charges[1, 0, k], 0) - jnp.where(col_block == k, charges[2, 0, k], 0)
    mask[...] = jnp.where((total & 3) == 0, 1.0, 0.0).astype(BF)

    side = slab * slab
    to = lax.broadcasted_iota(jnp.int32, (side, side), 0)
    frm = lax.broadcasted_iota(jnp.int32, (side, side), 1)
    perm[...] = jnp.where((to // slab == frm % slab) & (to % slab == frm // slab), 1.0, 0.0).astype(BF)

    load.wait()

    def prepare(e, carry):
        piece = mm[:, rows(e), :] * mask[rows(e), :][None]
        mm[:, rows(e), :] = piece
        turned = dot(perm[...], piece.reshape(side, chi)).astype(BF)
        sendb[e] = turned.reshape(slab, slab, chi)
        return carry

    lax.fori_loop(0, n, prepare, 0, unroll=4)
    mb[:, mine, :] = sendb[me]

    pl.semaphore_wait(barrier, n + n * (LEVELS - 1))

    def post(src, dst, level, send, recv, to_slot, at):
        pltpu.make_async_remote_copy(
            src_ref=src, dst_ref=dst.at[level, mine], send_sem=send.at[level], recv_sem=recv.at[level],
            device_id=(to_slot, peer(at)), device_id_type=MESH,
        ).start()

    def drain(ref, sem):
        pltpu.make_async_copy(ref, ref, sem).wait()

    others = pl.ds(0, chi - slab)

    hand_on = pltpu.make_async_remote_copy(
        src_ref=leaf_op, dst_ref=zbuf, send_sem=z_send, recv_sem=z_recv,
        device_id=(ahead(1), me), device_id_type=MESH,
    )

    def publish(src, level):
        def own():
            for at in others_at:
                post(src, rbuf, level, r_send, r_recv, slot, at)

        def parent():
            for at in steps:
                post(src, lbuf, level, l_send, l_recv, ahead(2**level), at)

        if level == 1:
            parent()
            own()
        else:
            own()
            if level > 1:
                parent()
        rbuf[level, mine] = src[...]

    def exchange(c):
        part = pl.ds(c * per, per)

        for at in others_at:
            to_dev = peer(at)
            pltpu.make_async_remote_copy(
                src_ref=sendb.at[to_dev, part], dst_ref=mb.at[part, mine],
                send_sem=a2a_send.at[c], recv_sem=a2a_recv.at[c],
                device_id=(slot, to_dev), device_id_type=MESH,
            ).start()

    hand_on.start()
    publish(leaf_op, 0)
    exchange(0)
    hand_on.wait_recv()
    lbuf[0, mine] = zbuf[...]
    for at in others_at:
        post(zbuf, lbuf, 0, l_send, l_recv, slot, at)
    for c in range(1, CHUNKS):
        exchange(c)

    def flip(a, carry):
        vt[a] = mm[a].T
        return carry

    lax.fori_loop(0, slab, flip, 0, unroll=4)

    take_left = jnp.where(assign[0] != 1, 1.0, 0.0).astype(BF)
    take_right = jnp.where(assign[0] != 0, 1.0, 0.0).astype(BF)

    def contract(turned, plain, first, count):
        def step(i, carry):
            mixed = dot(turned[i], scaled[...]).astype(BF)
            acc[...] += dot(mixed, plain[i])
            return carry

        lax.fori_loop(first, first + count, step, 0, unroll=True)

    for level in range(LEVELS):
        drain(rbuf.at[level, others], r_recv.at[level])
        scaled[...] = rbuf[level] * take_right
        acc[...] = jnp.zeros_like(acc)
        contract(vt, mm, 0, slab)
        drain(lbuf.at[level] if level > 0 else lbuf.at[level, others], l_recv.at[level])
        scaled[...] = lbuf[level] * take_left
        if level == 0:
            for c in range(CHUNKS):
                drain(mb.at[pl.ds(c * per, per), others], a2a_recv.at[c])

                def turn(b, carry):
                    ut[b] = mb[b].T
                    return carry

                lax.fori_loop(c * per, (c + 1) * per, turn, 0, unroll=True)
                contract(ut, mb, c * per, per)
        else:
            contract(ut, mb, 0, slab)

        rss[level] = acc[...].astype(BF)
        for at in others_at:
            to_dev = peer(at)
            pltpu.make_async_remote_copy(
                src_ref=rss.at[level, rows(to_dev)], dst_ref=rsr.at[level, me],
                send_sem=s_send.at[level], recv_sem=s_recv.at[level],
                device_id=(slot, to_dev), device_id_type=MESH,
            ).start()
        rsr[level, me] = rss[level, mine]
        drain(rsr.at[level, pl.ds(0, n - 1)], s_recv.at[level])
        whole = rsr[level, 0].astype(F32)
        for i in range(1, n):
            whole = whole + rsr[level, i].astype(F32)
        if level < LEVELS - 1:
            xs[level] = whole.astype(BF)
            publish(xs.at[level], level + 1)
        else:
            out[...] = whole.astype(BF)

    hand_on.wait_send()
    for c in range(CHUNKS):
        drain(mb.at[pl.ds(c * per, per), others], a2a_send.at[c])
    for level in range(LEVELS):
        drain(rbuf.at[level, others], r_send.at[level])
        drain(lbuf.at[level] if level > 0 else lbuf.at[level, others], l_send.at[level])
        drain(rsr.at[level, pl.ds(0, n - 1)], s_send.at[level])


def shards(isometries, leaf_ops, charges, assign):
    iso = isometries[0]
    slab, chi, _ = iso.shape
    n = lax.axis_size("bond")
    leaves = lax.axis_size("leaf")
    sem = pltpu.SemaphoreType.DMA
    result = pl.pallas_call(
        functools.partial(kernel, n, leaves),
        out_shape=jax.ShapeDtypeStruct((slab, chi), BF),
        in_specs=[
            pl.BlockSpec(memory_space=pl.ANY),
            pl.BlockSpec(memory_space=pltpu.VMEM),
            pl.BlockSpec(memory_space=pltpu.SMEM),
            pl.BlockSpec(memory_space=pltpu.SMEM),
        ],
        out_specs=pl.BlockSpec(memory_space=pltpu.VMEM),
        scratch_shapes=[
            pltpu.VMEM((slab, chi, chi), BF),
            pltpu.VMEM((n, slab, slab, chi), BF),
            pltpu.VMEM((slab, chi, chi), BF),
            pltpu.VMEM((slab, chi, chi), BF),
            pltpu.VMEM((slab, chi, chi), BF),
            pltpu.VMEM((chi, chi), BF),
            pltpu.VMEM((slab * slab, slab * slab), BF),
            pltpu.VMEM((chi, chi), BF),
            pltpu.VMEM((chi, chi), F32),
            pltpu.VMEM((LEVELS, slab, chi), BF),
            pltpu.VMEM((LEVELS, chi, chi), BF),
            pltpu.VMEM((LEVELS, chi, chi), BF),
            pltpu.VMEM((slab, chi), BF),
            pltpu.VMEM((LEVELS, chi, chi), BF),
            pltpu.VMEM((LEVELS, n, slab, chi), BF),
            sem,
            sem((CHUNKS,)), sem((CHUNKS,)),
            sem((LEVELS,)), sem((LEVELS,)),
            sem((LEVELS,)), sem((LEVELS,)),
            sem, sem,
            sem((LEVELS,)), sem((LEVELS,)),
        ],
        compiler_params=pltpu.CompilerParams(collective_id=0, has_side_effects=True),
    )(iso, leaf_ops[0, 0], jnp.transpose(charges, (1, 0, 2)), assign[0])
    return result[None, None]


def solution(mesh):
    in_specs = (
        P("leaf", "bond", None, None),
        P("leaf", None, "bond", None),
        P("leaf", None, None),
        P("leaf", None),
    )
    out_specs = P("leaf", None, "bond", None)
    return jax.shard_map(shards, mesh=mesh, in_specs=in_specs, out_specs=out_specs, check_vma=False)
```

```python
import functools
import math

import jax
import jax.numpy as jnp
from jax import lax
from jax.experimental import pallas as pl
from jax.experimental.pallas import tpu as pltpu
from jax.sharding import PartitionSpec as P

NBLK = 4
LEVELS = 3
CHUNKS = 4
BF = jnp.bfloat16
F32 = jnp.float32
MESH = pl.DeviceIdType.MESH


def dot(a, b):
    return jnp.dot(a, b, preferred_element_type=F32)


def kernel(
    n, leaves, iso, leaf_op, charges, assign, out,
    mm, sendb, mb, vt, ut, mask, perm, scaled, acc, xs, rbuf, lbuf, zbuf, rss, rsr,
    load_sem, a2a_send, a2a_recv, r_send, r_recv, l_send, l_recv, z_send, z_recv, s_send, s_recv,
):
    slab, chi, _ = iso.shape
    block = chi // NBLK
    per = slab // CHUNKS
    me = lax.axis_index("bond")
    slot = lax.axis_index("leaf")

    width = math.isqrt(n)
    steps = sorted(
        ((i, j) for i in range(width) for j in range(width)),
        key=lambda at: -sum(min(k, width - k) for k in at),
    )
    others_at = steps[:-1]

    def peer(at):
        return lax.rem(me // width + at[0], width) * width + lax.rem(lax.rem(me, width) + at[1], width)

    def ahead(by):
        return lax.rem(slot + by, leaves)

    def rows(i):
        return pl.ds(pl.multiple_of(i * slab, slab), slab)

    mine = rows(me)

    span = chi // NBLK
    loads = [
        pltpu.make_async_copy(iso.at[:, pl.ds(k * span, span)], mm.at[:, pl.ds(k * span, span)], load_sem.at[k])
        for k in range(NBLK)
    ]
    for load in loads:
        load.start()

    barrier = pltpu.get_barrier_semaphore()

    for at in others_at:
        pl.semaphore_signal(barrier, inc=1, device_id=(slot, peer(at)), device_id_type=MESH)
    pl.semaphore_signal(barrier, inc=1, device_id=(ahead(leaves - 1), me), device_id_type=MESH)
    for level in range(1, LEVELS):
        for at in steps:
            pl.semaphore_signal(
                barrier, inc=1, device_id=(ahead(leaves - 2**level), peer(at)), device_id_type=MESH
            )

    down = lax.broadcasted_iota(jnp.int32, (chi, 1), 0) // block
    across = lax.broadcasted_iota(jnp.int32, (1, chi), 1) // block
    left_right = jnp.zeros((chi, 1), jnp.int32) + charges[0, 0, (me * slab) // block]
    parent = jnp.zeros((1, chi), jnp.int32)
    for k in range(NBLK):
        left_right = left_right + jnp.where(down == k, charges[1, 0, k], 0)
        parent = parent + jnp.where(across == k, charges[2, 0, k], 0)
    mask[...] = jnp.where(((left_right - parent) & 3) == 0, 1.0, 0.0).astype(BF)

    side = slab * slab
    to = lax.broadcasted_iota(jnp.int32, (side, 1), 0)
    frm = lax.broadcasted_iota(jnp.int32, (1, side), 1)
    perm[...] = jnp.where(to // slab + to % slab * slab == frm, 1.0, 0.0).astype(BF)


    def prepare(e, carry):
        piece = mm[:, rows(e), :] * mask[rows(e), :][None]
        mm[:, rows(e), :] = piece
        turned = dot(perm[...], piece.reshape(side, chi)).astype(BF)
        sendb[e] = turned.reshape(slab, slab, chi)
        return carry

    for k, load in enumerate(loads):
        load.wait()
        lax.fori_loop(k * n // NBLK, (k + 1) * n // NBLK, prepare, 0, unroll=True)
    mb[:, mine, :] = sendb[me]

    pl.semaphore_wait(barrier, n + n * (LEVELS - 1))

    def post(src, dst, level, send, recv, to_slot, at):
        pltpu.make_async_remote_copy(
            src_ref=src, dst_ref=dst.at[level, mine], send_sem=send.at[level], recv_sem=recv.at[level],
            device_id=(to_slot, peer(at)), device_id_type=MESH,
        ).start()

    def drain(ref, sem):
        pltpu.make_async_copy(ref, ref, sem).wait()

    others = pl.ds(0, chi - slab)

    hand_on = pltpu.make_async_remote_copy(
        src_ref=leaf_op, dst_ref=zbuf, send_sem=z_send, recv_sem=z_recv,
        device_id=(ahead(1), me), device_id_type=MESH,
    )

    def publish(src, level):
        for at in steps:
            if level > 0:
                post(src, lbuf, level, l_send, l_recv, ahead(2**level), at)
            if at != (0, 0):
                post(src, rbuf, level, r_send, r_recv, slot, at)
        rbuf[level, mine] = src[...]

    def exchange(c):
        part = pl.ds(c * per, per)

        for at in others_at:
            to_dev = peer(at)
            pltpu.make_async_remote_copy(
                src_ref=sendb.at[to_dev, part], dst_ref=mb.at[part, mine],
                send_sem=a2a_send.at[c], recv_sem=a2a_recv.at[c],
                device_id=(slot, to_dev), device_id_type=MESH,
            ).start()

    hand_on.start()
    publish(leaf_op, 0)
    exchange(0)
    hand_on.wait_recv()
    lbuf[0, mine] = zbuf[...]
    for at in others_at:
        post(zbuf, lbuf, 0, l_send, l_recv, slot, at)
    for c in range(1, CHUNKS):
        exchange(c)

    def flip(a, carry):
        vt[a] = mm[a].T
        return carry

    lax.fori_loop(0, slab, flip, 0, unroll=4)

    take_left = jnp.where(assign[0] != 1, 1.0, 0.0).astype(BF)
    take_right = jnp.where(assign[0] != 0, 1.0, 0.0).astype(BF)

    def contract(turned, plain, first, count):
        def step(i, carry):
            mixed = dot(turned[i], scaled[...]).astype(BF)
            acc[...] += dot(mixed, plain[i])
            return carry

        lax.fori_loop(first, first + count, step, 0, unroll=True)

    for level in range(LEVELS):
        drain(rbuf.at[level, others], r_recv.at[level])
        scaled[...] = rbuf[level] * take_right
        acc[...] = jnp.zeros_like(acc)
        contract(vt, mm, 0, slab)
        drain(lbuf.at[level] if level > 0 else lbuf.at[level, others], l_recv.at[level])
        scaled[...] = lbuf[level] * take_left
        if level == 0:
            for c in range(CHUNKS):
                drain(mb.at[pl.ds(c * per, per), others], a2a_recv.at[c])

                def turn(b, carry):
                    ut[b] = mb[b].T
                    return carry

                lax.fori_loop(c * per, (c + 1) * per, turn, 0, unroll=True)
                contract(ut, mb, c * per, per)
        else:
            contract(ut, mb, 0, slab)

        rss[level] = acc[...].astype(BF)
        for at in others_at:
            to_dev = peer(at)
            pltpu.make_async_remote_copy(
                src_ref=rss.at[level, rows(to_dev)], dst_ref=rsr.at[level, me],
                send_sem=s_send.at[level], recv_sem=s_recv.at[level],
                device_id=(slot, to_dev), device_id_type=MESH,
            ).start()
        rsr[level, me] = rss[level, mine]
        drain(rsr.at[level, pl.ds(0, n - 1)], s_recv.at[level])
        whole = rsr[level, 0].astype(F32)
        for i in range(1, n):
            whole = whole + rsr[level, i].astype(F32)
        if level < LEVELS - 1:
            xs[level] = whole.astype(BF)
            publish(xs.at[level], level + 1)
        else:
            out[...] = whole.astype(BF)

    hand_on.wait_send()
    for c in range(CHUNKS):
        drain(mb.at[pl.ds(c * per, per), others], a2a_send.at[c])
    for level in range(LEVELS):
        drain(rbuf.at[level, others], r_send.at[level])
        drain(lbuf.at[level] if level > 0 else lbuf.at[level, others], l_send.at[level])
        drain(rsr.at[level, pl.ds(0, n - 1)], s_send.at[level])


def place(src, dst, done):
    copy = pltpu.make_async_copy(src, dst, done)
    copy.start()
    copy.wait()


def shards(isometries, leaf_ops, charges, assign):
    iso = isometries[0]
    slab, chi, _ = iso.shape
    n = lax.axis_size("bond")
    leaves = lax.axis_size("leaf")
    sem = pltpu.SemaphoreType.DMA
    result = pl.pallas_call(
        functools.partial(kernel, n, leaves),
        out_shape=jax.ShapeDtypeStruct((slab, chi), BF),
        in_specs=[
            pl.BlockSpec(memory_space=pl.ANY),
            pl.BlockSpec(memory_space=pltpu.VMEM),
            pl.BlockSpec(memory_space=pltpu.SMEM),
            pl.BlockSpec(memory_space=pltpu.SMEM),
        ],
        out_specs=pl.BlockSpec(memory_space=pltpu.VMEM),
        scratch_shapes=[
            pltpu.VMEM((slab, chi, chi), BF),
            pltpu.VMEM((n, slab, slab, chi), BF),
            pltpu.VMEM((slab, chi, chi), BF),
            pltpu.VMEM((slab, chi, chi), BF),
            pltpu.VMEM((slab, chi, chi), BF),
            pltpu.VMEM((chi, chi), BF),
            pltpu.VMEM((slab * slab, slab * slab), BF),
            pltpu.VMEM((chi, chi), BF),
            pltpu.VMEM((chi, chi), F32),
            pltpu.VMEM((LEVELS, slab, chi), BF),
            pltpu.VMEM((LEVELS, chi, chi), BF),
            pltpu.VMEM((LEVELS, chi, chi), BF),
            pltpu.VMEM((slab, chi), BF),
            pltpu.VMEM((LEVELS, chi, chi), BF),
            pltpu.VMEM((LEVELS, n, slab, chi), BF),
            sem((NBLK,)),
            sem((CHUNKS,)), sem((CHUNKS,)),
            sem((LEVELS,)), sem((LEVELS,)),
            sem((LEVELS,)), sem((LEVELS,)),
            sem, sem,
            sem((LEVELS,)), sem((LEVELS,)),
        ],
        compiler_params=pltpu.CompilerParams(collective_id=0, has_side_effects=True),
    )(iso, leaf_ops[0, 0], jnp.transpose(charges, (1, 0, 2)), assign[0])
    result = pl.pallas_call(
        place,
        out_shape=jax.ShapeDtypeStruct((slab, chi), BF),
        in_specs=[pl.BlockSpec(memory_space=pl.ANY)],
        out_specs=pl.BlockSpec(memory_space=pl.ANY),
        scratch_shapes=[sem],
    )(result)
    return result[None, None]


def solution(mesh):
    in_specs = (
        P("leaf", "bond", None, None),
        P("leaf", None, "bond", None),
        P("leaf", None, None),
        P("leaf", None),
    )
    out_specs = P("leaf", None, "bond", None)
    return jax.shard_map(shards, mesh=mesh, in_specs=in_specs, out_specs=out_specs, check_vma=False)
```

```python
import functools
import math

import jax
import jax.numpy as jnp
from jax import lax
from jax.experimental import pallas as pl
from jax.experimental.pallas import tpu as pltpu
from jax.sharding import PartitionSpec as P

NBLK = 4
LEVELS = 3
CHUNKS = 4
VMEM_MIB = 48
BF = jnp.bfloat16
F32 = jnp.float32
MESH = pl.DeviceIdType.MESH


def dot(a, b):
    return jnp.dot(a, b, preferred_element_type=F32)


def kernel(
    n, leaves, iso, leaf_op, charges, assign, out,
    mm, sendb, mb, vt, ut, mask, perm, scaled, acc, xs, rbuf, lbuf, zbuf, rss, rsr,
    load_sem, a2a_send, a2a_recv, r_send, r_recv, l_send, l_recv, z_send, z_recv, s_send, s_recv,
):
    slab, chi, _ = iso.shape
    block = chi // NBLK
    per = slab // CHUNKS
    me = lax.axis_index("bond")
    slot = lax.axis_index("leaf")

    width = math.isqrt(n)
    steps = sorted(
        ((i, j) for i in range(width) for j in range(width)),
        key=lambda at: -sum(min(k, width - k) for k in at),
    )
    others_at = steps[:-1]

    def peer(at):
        return lax.rem(me // width + at[0], width) * width + lax.rem(lax.rem(me, width) + at[1], width)

    def ahead(by):
        return lax.rem(slot + by, leaves)

    def rows(i):
        return pl.ds(pl.multiple_of(i * slab, slab), slab)

    mine = rows(me)

    load = pltpu.make_async_copy(iso, mm, load_sem)
    load.start()

    barrier = pltpu.get_barrier_semaphore()

    for at in others_at:
        pl.semaphore_signal(barrier, inc=1, device_id=(slot, peer(at)), device_id_type=MESH)
    pl.semaphore_signal(barrier, inc=1, device_id=(ahead(leaves - 1), me), device_id_type=MESH)
    for level in range(1, LEVELS):
        for at in steps:
            pl.semaphore_signal(
                barrier, inc=1, device_id=(ahead(leaves - 2**level), peer(at)), device_id_type=MESH
            )

    row_block = lax.broadcasted_iota(jnp.int32, (chi, chi), 0) // block
    col_block = lax.broadcasted_iota(jnp.int32, (chi, chi), 1) // block
    total = jnp.zeros((chi, chi), jnp.int32) + charges[0, 0, (me * slab) // block]
    for k in range(NBLK):
        total = total + jnp.where(row_block == k, charges[1, 0, k], 0) - jnp.where(col_block == k, charges[2, 0, k], 0)
    mask[...] = jnp.where((total & 3) == 0, 1.0, 0.0).astype(BF)

    side = slab * slab
    to = lax.broadcasted_iota(jnp.int32, (side, side), 0)
    frm = lax.broadcasted_iota(jnp.int32, (side, side), 1)
    perm[...] = jnp.where((to // slab == frm % slab) & (to % slab == frm // slab), 1.0, 0.0).astype(BF)

    load.wait()

    def prepare(e, carry):
        piece = mm[:, rows(e), :] * mask[rows(e), :][None]
        mm[:, rows(e), :] = piece
        turned = dot(perm[...], piece.reshape(side, chi)).astype(BF)
        sendb[e] = turned.reshape(slab, slab, chi)
        return carry

    lax.fori_loop(0, n, prepare, 0, unroll=4)
    mb[:, mine, :] = sendb[me]

    pl.semaphore_wait(barrier, n + n * (LEVELS - 1))

    def post(src, dst, level, send, recv, to_slot, at):
        pltpu.make_async_remote_copy(
            src_ref=src, dst_ref=dst.at[level, mine], send_sem=send.at[level], recv_sem=recv.at[level],
            device_id=(to_slot, peer(at)), device_id_type=MESH,
        ).start()

    def drain(ref, sem):
        pltpu.make_async_copy(ref, ref, sem).wait()

    others = pl.ds(0, chi - slab)

    hand_on = pltpu.make_async_remote_copy(
        src_ref=leaf_op, dst_ref=zbuf, send_sem=z_send, recv_sem=z_recv,
        device_id=(ahead(1), me), device_id_type=MESH,
    )

    def publish(src, level):
        for at in steps:
            if level > 0:
                post(src, lbuf, level, l_send, l_recv, ahead(2**level), at)
            if at != (0, 0):
                post(src, rbuf, level, r_send, r_recv, slot, at)
        rbuf[level, mine] = src[...]

    def exchange(c):
        part = pl.ds(c * per, per)

        for at in others_at:
            to_dev = peer(at)
            pltpu.make_async_remote_copy(
                src_ref=sendb.at[to_dev, part], dst_ref=mb.at[part, mine],
                send_sem=a2a_send.at[c], recv_sem=a2a_recv.at[c],
                device_id=(slot, to_dev), device_id_type=MESH,
            ).start()

    hand_on.start()
    publish(leaf_op, 0)
    exchange(0)
    hand_on.wait_recv()
    lbuf[0, mine] = zbuf[...]
    for at in others_at:
        post(zbuf, lbuf, 0, l_send, l_recv, slot, at)
    for c in range(1, CHUNKS):
        exchange(c)

    def flip(a, carry):
        vt[a] = mm[a].T
        return carry

    lax.fori_loop(0, slab, flip, 0, unroll=4)

    take_left = jnp.where(assign[0] != 1, 1.0, 0.0).astype(BF)
    take_right = jnp.where(assign[0] != 0, 1.0, 0.0).astype(BF)

    def contract(turned, plain, first, count):
        def step(i, carry):
            mixed = dot(turned[i], scaled[...]).astype(BF)
            acc[...] += dot(mixed, plain[i])
            return carry

        lax.fori_loop(first, first + count, step, 0, unroll=True)

    for level in range(LEVELS):
        drain(rbuf.at[level, others], r_recv.at[level])
        scaled[...] = rbuf[level] * take_right
        acc[...] = jnp.zeros_like(acc)
        contract(vt, mm, 0, slab)
        drain(lbuf.at[level] if level > 0 else lbuf.at[level, others], l_recv.at[level])
        scaled[...] = lbuf[level] * take_left
        if level == 0:
            for c in range(CHUNKS):
                drain(mb.at[pl.ds(c * per, per), others], a2a_recv.at[c])

                def turn(b, carry):
                    ut[b] = mb[b].T
                    return carry

                lax.fori_loop(c * per, (c + 1) * per, turn, 0, unroll=True)
                contract(ut, mb, c * per, per)
        else:
            contract(ut, mb, 0, slab)

        rss[level] = acc[...].astype(BF)
        for at in others_at:
            to_dev = peer(at)
            pltpu.make_async_remote_copy(
                src_ref=rss.at[level, rows(to_dev)], dst_ref=rsr.at[level, me],
                send_sem=s_send.at[level], recv_sem=s_recv.at[level],
                device_id=(slot, to_dev), device_id_type=MESH,
            ).start()
        rsr[level, me] = rss[level, mine]
        drain(rsr.at[level, pl.ds(0, n - 1)], s_recv.at[level])
        whole = rsr[level, 0].astype(F32)
        for i in range(1, n):
            whole = whole + rsr[level, i].astype(F32)
        if level < LEVELS - 1:
            xs[level] = whole.astype(BF)
            publish(xs.at[level], level + 1)
        else:
            out[...] = whole

    hand_on.wait_send()
    for c in range(CHUNKS):
        drain(mb.at[pl.ds(c * per, per), others], a2a_send.at[c])
    for level in range(LEVELS):
        drain(rbuf.at[level, others], r_send.at[level])
        drain(lbuf.at[level] if level > 0 else lbuf.at[level, others], l_send.at[level])
        drain(rsr.at[level, pl.ds(0, n - 1)], s_send.at[level])


def hbm(x):
    return pltpu.with_memory_space_constraint(x, pltpu.HBM)


def shards(isometries, leaf_ops, charges, assign):
    iso = isometries[0]
    slab, chi, _ = iso.shape
    n = lax.axis_size("bond")
    leaves = lax.axis_size("leaf")
    sem = pltpu.SemaphoreType.DMA
    result = pl.pallas_call(
        functools.partial(kernel, n, leaves),
        out_shape=jax.ShapeDtypeStruct((slab, chi), F32),
        in_specs=[
            pl.BlockSpec(memory_space=pl.ANY),
            pl.BlockSpec(memory_space=pltpu.VMEM),
            pl.BlockSpec(memory_space=pltpu.SMEM),
            pl.BlockSpec(memory_space=pltpu.SMEM),
        ],
        out_specs=pl.BlockSpec(memory_space=pltpu.VMEM),
        scratch_shapes=[
            pltpu.VMEM((slab, chi, chi), BF),
            pltpu.VMEM((n, slab, slab, chi), BF),
            pltpu.VMEM((slab, chi, chi), BF),
            pltpu.VMEM((slab, chi, chi), BF),
            pltpu.VMEM((slab, chi, chi), BF),
            pltpu.VMEM((chi, chi), BF),
            pltpu.VMEM((slab * slab, slab * slab), BF),
            pltpu.VMEM((chi, chi), BF),
            pltpu.VMEM((chi, chi), F32),
            pltpu.VMEM((LEVELS, slab, chi), BF),
            pltpu.VMEM((LEVELS, chi, chi), BF),
            pltpu.VMEM((LEVELS, chi, chi), BF),
            pltpu.VMEM((slab, chi), BF),
            pltpu.VMEM((LEVELS, chi, chi), BF),
            pltpu.VMEM((LEVELS, n, slab, chi), BF),
            sem,
            sem((CHUNKS,)), sem((CHUNKS,)),
            sem((LEVELS,)), sem((LEVELS,)),
            sem((LEVELS,)), sem((LEVELS,)),
            sem, sem,
            sem((LEVELS,)), sem((LEVELS,)),
        ],
        compiler_params=pltpu.CompilerParams(collective_id=0, has_side_effects=True, vmem_limit_bytes=VMEM_MIB * 2**20),
    )(hbm(iso), hbm(leaf_ops[0, 0]), hbm(jnp.transpose(charges, (1, 0, 2))), assign[0])
    return result.astype(BF)[None, None]


def solution(mesh):
    in_specs = (
        P("leaf", "bond", None, None),
        P("leaf", None, "bond", None),
        P("leaf", None, None),
        P("leaf", None),
    )
    out_specs = P("leaf", None, "bond", None)
    return jax.shard_map(shards, mesh=mesh, in_specs=in_specs, out_specs=out_specs, check_vma=False)
```
